256 devices in a mesh: dp: 32 (over y, z_hi, core), code: 8 (over x, z_lo).
Axes of the slice: x: 4, y: 4, z: 8 (z_hi: 4, z_lo: 2; z = z_hi * 2 + z_lo), core: 2. Of those that a mesh axis runs over, the one named last changes fastest.
Arguments:
- encoded: bfloat16 [8192, 256], P('dp'), may hold values from -32 to 32
- codebook: bfloat16 [131072, 256], P('code'), may hold values from -2 to 2
Outputs:
- grad_rows: float32 [8192, 256], P('dp')
- grad_codes: float32 [131072, 256], P(('code', 'dp'))
The draws below stay inside these ranges and needn't reach their ends.
All inputs are finite; a program needn't handle non-finite values.
Results may differ from the reference program's by a relative error of at most 0.0045.
Values may be sent and summed in bfloat16 or wider, within the bound.
A program may use at most 64 MiB of HBM per device.

```python
import math
import jax
import jax.numpy as jnp
from jax import lax

D = 256
CODES = 131072
ROWS = 8192


def common_codebook(key):
    values = jax.random.normal(jax.random.fold_in(key, 7), (CODES, D), jnp.float32) * 0.25
    return jnp.clip(values, -2.0, 2.0)


def draw_codebook(key, part):
    return common_codebook(key).astype(jnp.bfloat16)


def draw_encoded(key, part):
    enc_key = jax.random.fold_in(key, 11)
    code_table = common_codebook(key)
    values = jax.random.normal(enc_key, (ROWS, D), jnp.float32)
    chosen = jax.random.randint(jax.random.fold_in(enc_key, 3), (12,), 0, ROWS)
    earlier = jax.random.randint(jax.random.fold_in(enc_key, 4), (12,), 0, CODES)
    later = jax.random.randint(jax.random.fold_in(enc_key, 5), (12,), 0, CODES)
    strength = jnp.tile(jnp.array([20.0, 26.0, 32.0], jnp.float32), 4)
    aligned = strength[:, None] * jnp.tanh(4.0 * (code_table[earlier] + code_table[later]))
    values = values.at[chosen].set(aligned)
    return jnp.clip(values, -32.0, 32.0).astype(jnp.bfloat16)


def setup_inputs(seed: int = 0) -> dict:
    streams_of = jax.random.split(jax.random.key(seed), 3)
    return {
        "encoded": draw_encoded(jax.random.fold_in(streams_of[2], 71), 0),
        "codebook": draw_codebook(jax.random.fold_in(streams_of[2], 71), 0),
    }


def logit_block(encoded, code_rows, code_squares):
    scores = lax.dot_general(encoded, code_rows, (((1,), (1,)), ((), ())), preferred_element_type=jnp.float32)
    return scores - 0.5 * code_squares[None, :]


def grad_block(encoded, row_lse, entropy, cross_term, code_rows, code_squares, log_mass):
    logits = logit_block(encoded, code_rows, code_squares)
    weights = jnp.exp(logits - row_lse[:, None])
    shaped = weights * (row_lse[:, None] - logits - entropy[:, None] + log_mass[None, :] - cross_term[:, None])
    return shaped.astype(jnp.bfloat16)


def code_term(grad_tile, encoded, code_rows):
    pulled = lax.dot_general(grad_tile, encoded, (((0,), (0,)), ((), ())), preferred_element_type=jnp.float32)
    totals = jnp.sum(grad_tile.astype(jnp.float32), axis=0)
    return pulled - totals[:, None] * code_rows.astype(jnp.float32)


def reference(encoded, codebook):
    squares = jnp.sum(jnp.square(codebook.astype(jnp.float32)), axis=1)
    block_size = math.gcd(CODES, 4096)
    block_count = CODES // block_size
    code_blocks = codebook.reshape(block_count, block_size, D)
    square_blocks = squares.reshape(block_count, block_size)

    def max_of(inputs):
        return jnp.max(logit_block(encoded, inputs[0], inputs[1]), axis=1)

    row_max = jnp.max(lax.map(max_of, (code_blocks, square_blocks)), axis=0)

    def sums_of(inputs):
        logits = logit_block(encoded, inputs[0], inputs[1])
        exponent = jnp.exp(logits - row_max[:, None])
        return jnp.sum(exponent, axis=1), jnp.sum(exponent * logits, axis=1)

    block_sums, block_dots = lax.map(sums_of, (code_blocks, square_blocks))
    row_sum = jnp.sum(block_sums, axis=0)
    row_dot = jnp.sum(block_dots, axis=0)
    row_lse = row_max + jnp.log(row_sum)
    entropy = row_lse - row_dot / row_sum

    def mass_of(inputs):
        logits = logit_block(encoded, inputs[0], inputs[1])
        return jnp.sum(jnp.exp(logits - row_lse[:, None]), axis=0)

    mean_mass = lax.map(mass_of, (code_blocks, square_blocks)).reshape(CODES) / ROWS
    log_mass = jnp.log(mean_mass)
    log_blocks = log_mass.reshape(block_count, block_size)

    def cross_of(inputs):
        logits = logit_block(encoded, inputs[0], inputs[1])
        weights = jnp.exp(logits - row_lse[:, None])
        return jnp.sum(weights * inputs[2][None, :], axis=1)

    cross_term = jnp.sum(lax.map(cross_of, (code_blocks, square_blocks, log_blocks)), axis=0)

    def grad_step(running, inputs):
        grad_tile = grad_block(encoded, row_lse, entropy, cross_term, inputs[0], inputs[1], inputs[2])
        added = running + jnp.dot(grad_tile, inputs[0], preferred_element_type=jnp.float32)
        return added, code_term(grad_tile, encoded, inputs[0])

    grad_rows, terms = lax.scan(grad_step, jnp.zeros((ROWS, D), jnp.float32), (code_blocks, square_blocks, log_blocks))
    return grad_rows, terms.reshape(CODES, D)
```

```python
import functools

import jax
import jax.numpy as jnp
from jax import lax
from jax.experimental import pallas as pl
from jax.experimental.pallas import tpu as pltpu
from jax.sharding import PartitionSpec as P

NX, NY, NZH, NZL, NC = 4, 4, 4, 2, 2
F32, BF16 = jnp.float32, jnp.bfloat16
LANES = 128


def remote(src, dst, send_sem, recv_sem, device):
    return pltpu.make_async_remote_copy(
        src_ref=src,
        dst_ref=dst,
        send_sem=send_sem,
        recv_sem=recv_sem,
        device_id=device,
        device_id_type=pl.DeviceIdType.MESH,
    )


class Share:
    def __init__(self, buf, n, me, device_of, send_sem, recv_sem):
        self.buf, self.n, self.me, self.device_of = buf, n, me, device_of
        self.send_sem, self.recv_sem = send_sem, recv_sem

    def start(self):
        for r in range(1, self.n):
            remote(
                self.buf.at[self.me],
                self.buf.at[self.me],
                self.send_sem.at[r],
                self.recv_sem.at[self.me],
                self.device_of(lax.rem(self.me + r, self.n)),
            ).start()

    def wait_recv(self):
        for r in range(1, self.n):
            other = lax.rem(self.me + r, self.n)
            remote(
                self.buf.at[other],
                self.buf.at[other],
                self.send_sem.at[r],
                self.recv_sem.at[other],
                self.device_of(other),
            ).wait_recv()

    def wait_send(self):
        for r in range(1, self.n):
            other = lax.rem(self.me + r, self.n)
            remote(
                self.buf.at[self.me],
                self.buf.at[self.me],
                self.send_sem.at[r],
                self.recv_sem.at[self.me],
                self.device_of(other),
            ).wait_send()


def transposed(block):
    return block.astype(F32).T.astype(BF16)


def kernel(
    rows_total,
    enc, book, rows_out, codes_out,
    cbt, et, eg, ct, hsq, logit, weight, tile, lane_sum, log_mass,
    stat_x, stat_z, lse8, t8, mass, t_x, t_z,
    grad_t, row_send, row_x, row_xsum, row_xsend, row_z, row_fin,
    code_own, code_send, code_core, code_ysend, code_y,
    book_sem, es_s, es_r, ef_s, ef_r, sx_s, sx_r, sz_s, sz_r, ms_s, ms_r,
    tx_s, tx_r, tz_s, tz_r, rx_s, rx_r, rz_s, rz_r, ra_s, ra_r, rb_s, rb_r,
    cc_s, cc_r, cy_s, cy_r,
):
    rows, feats = enc.shape
    tile_rows = rows * NZH
    chunk = cbt.shape[0] // NY
    half = chunk // NC
    rb = rows // LANES
    tb = tile_rows // LANES
    nz = NZH * NZL

    dp, code = lax.axis_index("dp"), lax.axis_index("code")
    y, zh, core = dp // (NZH * NC), lax.rem(dp // NC, NZH), lax.rem(dp, NC)
    x, zl = code // NZL, lax.rem(code, NZL)
    z = zh * NZL + zl
    yc = y * NC + core

    def device(x=x, y=y, zh=zh, zl=zl, core=core):
        return ((y * NZH + zh) * NC + core, x * NZL + zl)

    def at_x(i):
        return device(x=i)

    def at_z(i):
        return device(zh=i // NZL, zl=lax.rem(i, NZL))

    def at_y(i):
        return device(y=i)

    def at_yc(i):
        return device(y=i // NC, core=lax.rem(i, NC))

    def book_copy(r, c):
        start = pl.multiple_of((c * NZH + lax.rem(zh + r, NZH)) * chunk, chunk)
        if r == 0:
            target = cbt.at[pl.ds(c * chunk, chunk), :]
        else:
            target = tile.at[pl.ds(c * chunk, chunk), pl.ds((r - 1) * feats, feats)]
        return pltpu.make_async_copy(
            book.at[pl.ds(start, chunk), :], target, book_sem.at[r * NY + c]
        )

    for r in range(NZH):
        for c in range(NY):
            book_copy(r, c).start()

    barrier = pltpu.get_barrier_semaphore()
    partners = (
        [at_x(lax.rem(x + r, NX)) for r in range(1, NX)]
        + [at_z(lax.rem(z + r, nz)) for r in range(1, nz)]
        + [at_yc(lax.rem(yc + r, NY * NC)) for r in range(1, NY * NC)]
    )
    for partner in partners:
        pl.semaphore_signal(
            barrier, inc=1, device_id=partner, device_id_type=pl.DeviceIdType.MESH
        )

    own_lanes = pl.ds(pl.multiple_of(zh * rows, LANES), rows)
    own_t = transposed(enc[...])
    et[:, own_lanes] = own_t
    eg[zh] = enc[...]

    step = 128

    def online(r, c, state):
        def body(i, state):
            top, total = state
            start = pl.multiple_of(c * chunk + i * step, step)
            if r == 0:
                codes = cbt[pl.ds(start, step), :]
            else:
                codes = tile[pl.ds(start, step), pl.ds((r - 1) * feats, feats)]
            wide = codes.astype(F32)
            squared = wide * wide
            folded = squared[:, :LANES]
            for k in range(1, feats // LANES):
                folded = folded + squared[:, k * LANES:(k + 1) * LANES]
            halved = 0.5 * jnp.sum(folded, axis=1, keepdims=True)
            if r == 0:
                hsq[pl.ds(start, step), :] = jnp.broadcast_to(halved, (step, LANES))
            scores = jnp.dot(codes, et[:, own_lanes], preferred_element_type=F32)
            logits = (scores - halved).reshape(step // 8, 8, rows)
            new_top = jnp.maximum(top, jnp.max(logits, axis=0))
            total = total * jnp.exp(top - new_top) + jnp.sum(
                jnp.exp(logits - new_top[None]), axis=0
            )
            return new_top, total

        return lax.fori_loop(0, chunk // step, body, state, unroll=True)

    slice_rows = rows // NX
    my_slice = pl.ds(pl.multiple_of(x * slice_rows, slice_rows), slice_rows)

    def e_send(r):
        other = lax.rem(zh + r, NZH)
        return remote(
            enc.at[my_slice, :], eg.at[zh, my_slice, :], es_s.at[r], es_r.at[zh], device(zh=other)
        )

    def e_recv(r):
        other = lax.rem(zh + r, NZH)
        return remote(
            enc.at[my_slice, :], eg.at[other, my_slice, :], es_s.at[r], es_r.at[other],
            device(zh=other),
        )

    def e_forward(r, q):
        other = lax.rem(zh + r, NZH)
        part = eg.at[other, my_slice, :]
        return remote(
            part, part, ef_s.at[r * NX + q], ef_r.at[other * NX + x], at_x(lax.rem(x + q, NX))
        )

    def e_forwarded(r, q):
        other, xs = lax.rem(zh + r, NZH), lax.rem(x + q, NX)
        start = pl.multiple_of(xs * slice_rows, slice_rows)
        part = eg.at[other, pl.ds(start, slice_rows), :]
        return remote(part, part, ef_s.at[r * NX + q], ef_r.at[other * NX + xs], at_x(xs))

    state = (jnp.full((8, rows), -1e30, F32), jnp.zeros((8, rows), F32))
    for r in range(NZH):
        for c in range(NY):
            book_copy(r, c).wait()

        def chunks(c, state, r=r):
            return online(r, c, state)

        state = lax.fori_loop(0, NY, chunks, state)
        if r == 0:
            pl.semaphore_wait(barrier, len(partners))
            for k in range(1, NZH):
                e_send(k).start()
    top8, total8 = state
    top = jnp.max(top8, axis=0, keepdims=True)
    total = jnp.sum(total8 * jnp.exp(top8 - top), axis=0, keepdims=True)

    for k in range(rb):
        stat_x[x, k:k + 1, :] = top[:, k * LANES:(k + 1) * LANES]
        stat_x[x, rb + k:rb + k + 1, :] = total[:, k * LANES:(k + 1) * LANES]
    share_sx = Share(stat_x, NX, x, at_x, sx_s, sx_r)
    share_sx.start()

    for r in range(1, NZH):
        e_recv(r).wait_recv()
        for q in range(1, NX):
            e_forward(r, q).start()

    mm_step = 256 if chunk % 256 == 0 else 128

    def fill_logits(block):
        lanes = pl.ds(pl.multiple_of(block * rows, LANES), rows)

        def body(i, carry):
            at = pl.ds(pl.multiple_of(i * mm_step, mm_step), mm_step)
            scores = jnp.dot(cbt[at, :], et[:, lanes], preferred_element_type=F32)
            halved = hsq[at, :]
            for k in range(rb):
                lane = pl.ds(pl.multiple_of(block * rows + k * LANES, LANES), LANES)
                logit[at, lane] = scores[:, k * LANES:(k + 1) * LANES] - halved
            return carry

        lax.fori_loop(0, NY * chunk // mm_step, body, 0, unroll=2)

    fill_logits(zh)

    share_sx.wait_recv()
    tops, sums = stat_x[:, 0:rb, :], stat_x[:, rb:2 * rb, :]
    top = jnp.max(tops, axis=0)
    stat_z[z, 0:rb, :] = top
    stat_z[z, rb:2 * rb, :] = jnp.sum(sums * jnp.exp(tops - top[None]), axis=0)
    share_sz = Share(stat_z, nz, z, at_z, sz_s, sz_r)
    share_sz.start()

    def turn_codes(i, carry):
        at = pl.ds(pl.multiple_of(i * mm_step, mm_step), mm_step)
        ct[:, at] = transposed(cbt[at, :])
        return carry

    lax.fori_loop(0, NY * chunk // mm_step, turn_codes, 0)

    for r in range(1, NZH):
        other = lax.rem(zh + r, NZH)
        for q in range(1, NX):
            e_forwarded(r, q).wait_recv()
        et[:, pl.ds(pl.multiple_of(other * rows, LANES), rows)] = transposed(eg[other])
        fill_logits(other)

    share_sz.wait_recv()
    for b in range(NZH):
        tops = stat_z[b * NZL:(b + 1) * NZL, 0:rb, :]
        sums = stat_z[b * NZL:(b + 1) * NZL, rb:2 * rb, :]
        top = jnp.max(tops, axis=0)
        lse = top + jnp.log(jnp.sum(sums * jnp.exp(tops - top[None]), axis=0))
        for k in range(rb):
            lane = (b * rb + k) * LANES
            lse8[:, lane:lane + LANES] = jnp.broadcast_to(lse[k:k + 1, :], (8, LANES))

    el_step = 32
    mass_rows = chunk // LANES
    share_m = []
    for c in range(NY):
        def weigh(i, carry, c=c):
            at = pl.ds(pl.multiple_of(c * chunk + i * el_step, el_step), el_step)
            values = logit[at, :].reshape(el_step // 8, 8, tile_rows)
            log_weights = (values - lse8[...][None]).reshape(el_step, tile_rows)
            weights = jnp.exp(log_weights)
            logit[at, :] = log_weights
            weight[at, :] = weights
            part = weights[:, :LANES]
            for k in range(1, tb):
                part = part + weights[:, k * LANES:(k + 1) * LANES]
            lane_sum[at, :] = part
            return carry

        lax.fori_loop(0, chunk // el_step, weigh, 0, unroll=2)
        for k in range(mass_rows):
            start = c * chunk + k * LANES
            mass[c, yc, k:k + 1, :] = jnp.sum(
                lane_sum[start:start + LANES, :].T, axis=0, keepdims=True
            )
        share = Share(mass.at[c], NY * NC, yc, at_yc, ms_s.at[c], ms_r.at[c])
        share.start()
        share_m.append(share)

    t_sum = jnp.zeros((8, tile_rows), F32)
    for c in range(NY):
        share_m[c].wait_recv()
        logs = jnp.log(jnp.sum(mass[c], axis=0) / rows_total)
        for k in range(mass_rows):
            start = c * chunk + k * LANES
            log_mass[start:start + LANES, :] = jnp.broadcast_to(
                logs[k:k + 1, :], (LANES, LANES)
            ).T

        def shape(i, t_sum, c=c):
            at = pl.ds(pl.multiple_of(c * chunk + i * el_step, el_step), el_step)
            logs = log_mass[at, :]
            parts = []
            for k in range(tb):
                lane = slice(k * LANES, (k + 1) * LANES)
                q = weight[at, lane] * (logs - logit[at, lane])
                logit[at, lane] = q
                parts.append(jnp.sum(q.reshape(el_step // 8, 8, LANES), axis=0))
            return t_sum + jnp.concatenate(parts, axis=1)

        t_sum = lax.fori_loop(0, chunk // el_step, shape, t_sum, unroll=2)
    t_row = jnp.sum(t_sum, axis=0, keepdims=True)
    for k in range(tb):
        t_x[x, k:k + 1, :] = t_row[:, k * LANES:(k + 1) * LANES]
    share_tx = Share(t_x, NX, x, at_x, tx_s, tx_r)
    share_tx.start()
    share_tx.wait_recv()
    t_z[z] = jnp.sum(t_x[...], axis=0)
    share_tz = Share(t_z, nz, z, at_z, tz_s, tz_r)
    share_tz.start()
    share_tz.wait_recv()
    t_all = jnp.sum(t_z[...], axis=0)
    for k in range(tb):
        t8[:, k * LANES:(k + 1) * LANES] = jnp.broadcast_to(t_all[k:k + 1, :], (8, LANES))

    grad_t[...] = jnp.zeros_like(grad_t)
    g_step = 256 if chunk % 256 == 0 else 128

    def grads(i, carry):
        at = pl.ds(pl.multiple_of(i * g_step, g_step), g_step)
        sums = jnp.zeros((g_step, LANES), F32)
        for n in range(NZH):
            parts = []
            for k in range(rb):
                lane = slice(n * rows + k * LANES, n * rows + (k + 1) * LANES)
                q = logit[at, lane].reshape(g_step // 8, 8, LANES)
                w = weight[at, lane].reshape(g_step // 8, 8, LANES)
                g = (q - w * t8[:, lane][None]).reshape(g_step, LANES)
                sums = sums + g
                parts.append(g.astype(BF16))
            block = jnp.concatenate(parts, axis=1)
            lanes = slice(n * rows, (n + 1) * rows)
            tile[at, lanes] = block
            grad_t[:, lanes] += jnp.dot(ct[:, at], block, preferred_element_type=F32)
        lane_sum[at, :] = sums
        return carry

    lax.fori_loop(0, NY * chunk // g_step, grads, 0)

    fx = feats // NX
    fz = fx // NZL
    row_send[...] = grad_t[...].astype(BF16)

    def x_part(i):
        return pl.ds(pl.multiple_of(i * fx, fx), fx)

    def row_x_copy(r, sending):
        other = lax.rem(x + r, NX)
        slot = x if sending else other
        return remote(
            row_send.at[x_part(other), :], row_x.at[slot], rx_s.at[r], rx_r.at[slot], at_x(other)
        )

    for r in range(1, NX):
        row_x_copy(r, True).start()

    partner = 1 - core

    def code_core_copy(c):
        return remote(
            code_send.at[c], code_core.at[c], cc_s.at[c], cc_r.at[c], device(core=partner)
        )

    def code_y_copy(r, sending):
        other = lax.rem(y + r, NY)
        slot = y if sending else other
        return remote(
            code_ysend.at[r], code_y.at[slot], cy_s.at[r], cy_r.at[slot], at_y(other)
        )

    def code_block(other, owner):
        start = pl.multiple_of(other * chunk + owner * half, half)
        d_step = min(half, 256)
        out = []
        for k in range(half // d_step):
            at = pl.ds(pl.multiple_of(start + k * d_step, d_step), d_step)
            pulled = jnp.dot(
                tile[at, :], eg[...].reshape(tile_rows, feats), preferred_element_type=F32
            )
            totals = jnp.sum(lane_sum[at, :], axis=1, keepdims=True)
            out.append((k * d_step, d_step, pulled - totals * cbt[at, :].astype(F32)))
        return out

    def code_compute(r):
        other = lax.rem(y + r, NY)
        for start, size, value in code_block(other, partner):
            code_send[r, start:start + size, :] = value.astype(BF16)
        code_core_copy(r).start()
        for start, size, value in code_block(other, core):
            code_own[r, start:start + size, :] = value

    def code_forward(r):
        code_core_copy(r).wait_recv()
        code_ysend[r] = (code_own[r] + code_core[r].astype(F32)).astype(BF16)
        code_y_copy(r, True).start()

    order = sorted(range(1, NY), key=lambda r: -min(r, NY - r)) + [0]
    for i, r in enumerate(order):
        code_compute(r)
        if i >= 1:
            code_forward(order[i - 1])

    for r in range(1, NX):
        row_x_copy(r, False).wait_recv()
    total = grad_t[x_part(x), :]
    for r in range(1, NX):
        total = total + row_x[lax.rem(x + r, NX)].astype(F32)
    row_xsum[...] = total
    row_xsend[...] = total.astype(BF16)

    def z_piece(i):
        return (
            pl.ds(pl.multiple_of(lax.rem(i, NZL) * fz, fz), fz),
            pl.ds(pl.multiple_of((i // NZL) * rows, LANES), rows),
        )

    def row_z_copy(r, sending):
        other = lax.rem(z + r, nz)
        slot = z if sending else other
        return remote(
            row_xsend.at[z_piece(other)], row_z.at[slot], rz_s.at[r], rz_r.at[slot], at_z(other)
        )

    for r in range(1, nz):
        row_z_copy(r, True).start()

    code_core_copy(0).wait_recv()
    codes_out[...] = code_own[0] + code_core[0].astype(F32)

    for r in range(1, nz):
        row_z_copy(r, False).wait_recv()
    total = row_xsum[z_piece(z)]
    for r in range(1, nz):
        total = total + row_z[lax.rem(z + r, nz)].astype(F32)
    row_fin[x, zl] = total

    other_zl = 1 - zl
    mine = row_fin.at[x, zl]
    remote(mine, mine, ra_s, ra_r, device(zl=other_zl)).start()
    theirs = row_fin.at[x, other_zl]
    remote(theirs, theirs, ra_s, ra_r, device(zl=other_zl)).wait_recv()
    share_rb = Share(row_fin, NX, x, at_x, rb_s, rb_r)
    share_rb.start()

    for r in range(1, NY):
        code_y_copy(r, False).wait_recv()
    total = codes_out[...]
    for r in range(1, NY):
        total = total + code_y[lax.rem(y + r, NY)].astype(F32)
    codes_out[...] = total

    share_rb.wait_recv()
    rows_out[...] = row_fin[...].reshape(feats, rows).T

    for r in range(1, NZH):
        e_send(r).wait_send()
        for q in range(1, NX):
            e_forward(r, q).wait_send()
    for share in [share_sx, share_sz, share_tx, share_tz, share_rb] + share_m:
        share.wait_send()
    for r in range(1, NX):
        row_x_copy(r, True).wait_send()
    for r in range(1, nz):
        row_z_copy(r, True).wait_send()
    remote(mine, mine, ra_s, ra_r, device(zl=other_zl)).wait_send()
    for r in range(NY):
        code_core_copy(r).wait_send()
    for r in range(1, NY):
        code_y_copy(r, True).wait_send()


def body(encoded, codebook):
    rows, feats = encoded.shape
    shard = codebook.shape[0]
    tile_codes = shard // NZH
    chunk = tile_codes // NY
    half = chunk // NC
    tile_rows = rows * NZH
    rb, tb = rows // LANES, tile_rows // LANES
    nz = NZH * NZL
    fx = feats // NX
    fz = fx // NZL
    rows_total = rows * lax.axis_size("dp")
    dma = pltpu.SemaphoreType.DMA
    scratch = [
        pltpu.VMEM((tile_codes, feats), BF16),
        pltpu.VMEM((feats, tile_rows), BF16),
        pltpu.VMEM((NZH, rows, feats), BF16),
        pltpu.VMEM((feats, tile_codes), BF16),
        pltpu.VMEM((tile_codes, LANES), F32),
        pltpu.VMEM((tile_codes, tile_rows), F32),
        pltpu.VMEM((tile_codes, tile_rows), F32),
        pltpu.VMEM((tile_codes, tile_rows), BF16),
        pltpu.VMEM((tile_codes, LANES), F32),
        pltpu.VMEM((tile_codes, LANES), F32),
        pltpu.VMEM((NX, 2 * rb, LANES), F32),
        pltpu.VMEM((nz, 2 * rb, LANES), F32),
        pltpu.VMEM((8, tile_rows), F32),
        pltpu.VMEM((8, tile_rows), F32),
        pltpu.VMEM((NY, NY * NC, chunk // LANES, LANES), F32),
        pltpu.VMEM((NX, tb, LANES), F32),
        pltpu.VMEM((nz, tb, LANES), F32),
        pltpu.VMEM((feats, tile_rows), F32),
        pltpu.VMEM((feats, tile_rows), BF16),
        pltpu.VMEM((NX, fx, tile_rows), BF16),
        pltpu.VMEM((fx, tile_rows), F32),
        pltpu.VMEM((fx, tile_rows), BF16),
        pltpu.VMEM((nz, fz, rows), BF16),
        pltpu.VMEM((NX, NZL, fz, rows), F32),
        pltpu.VMEM((NY, half, feats), F32),
        pltpu.VMEM((NY, half, feats), BF16),
        pltpu.VMEM((NY, half, feats), BF16),
        pltpu.VMEM((NY, half, feats), BF16),
        pltpu.VMEM((NY, half, feats), BF16),
        dma((NZH * NY,)),
        dma((NZH,)), dma((NZH,)), dma((NZH * NX,)), dma((NZH * NX,)),
        dma((NX,)), dma((NX,)), dma((nz,)), dma((nz,)),
        dma((NY, NY * NC)), dma((NY, NY * NC)),
        dma((NX,)), dma((NX,)), dma((nz,)), dma((nz,)),
        dma((NX,)), dma((NX,)), dma((nz,)), dma((nz,)),
        dma, dma, dma((NX,)), dma((NX,)),
        dma((NY,)), dma((NY,)), dma((NY,)), dma((NY,)),
    ]
    vmem = pl.BlockSpec(memory_space=pltpu.VMEM)
    return pl.pallas_call(
        functools.partial(kernel, float(rows_total)),
        out_shape=(
            jax.ShapeDtypeStruct((rows, feats), F32),
            jax.ShapeDtypeStruct((half, feats), F32),
        ),
        in_specs=[vmem, pl.BlockSpec(memory_space=pl.ANY)],
        out_specs=(vmem, vmem),
        scratch_shapes=scratch,
        compiler_params=pltpu.CompilerParams(
            collective_id=0, has_side_effects=True, vmem_limit_bytes=67_000_000
        ),
    )(encoded, codebook)


def solution(mesh):
    placed = (P("dp", None), P("code", None))
    return jax.shard_map(
        body,
        mesh=mesh,
        in_specs=placed,
        out_specs=(P("dp", None), P(("code", "dp"), None)),
        check_vma=False,
    )
```

```python
import functools

import jax
import jax.numpy as jnp
from jax import lax
from jax.experimental import pallas as pl
from jax.experimental.pallas import tpu as pltpu
from jax.sharding import PartitionSpec as P

NX, NY, NZH, NZL, NC = 4, 4, 4, 2, 2
F32, BF16 = jnp.float32, jnp.bfloat16
LANES = 128


def remote(src, dst, send_sem, recv_sem, device):
    return pltpu.make_async_remote_copy(
        src_ref=src,
        dst_ref=dst,
        send_sem=send_sem,
        recv_sem=recv_sem,
        device_id=device,
        device_id_type=pl.DeviceIdType.MESH,
    )


class Copy:
    def __init__(self, log, outgoing, incoming):
        self.outgoing, self.incoming, self.arrived = outgoing, incoming, False
        outgoing.start()
        log.append(self)

    def recv(self):
        self.incoming.wait_recv()
        self.arrived = True

    def finish(self):
        if not self.arrived:
            self.recv()
        self.outgoing.wait_send()


class Share:
    def __init__(self, log, buf, n, me, device_of, send_sem, recv_sem):
        self.copies = []
        for r in range(1, n):
            there = lax.rem(me + r, n)

            def slot(i, r=r, there=there):
                return remote(
                    buf.at[i], buf.at[i], send_sem.at[r], recv_sem.at[i], device_of(there)
                )

            self.copies.append(Copy(log, slot(me), slot(there)))

    def recv(self):
        for copy in self.copies:
            copy.recv()


def transposed(block):
    return block.astype(F32).T.astype(BF16)


def kernel(
    rows_total,
    enc, book, rows_out, codes_out,
    cbt, et, eg, ct, hsq, logit, weight, tile, lane_sum, log_mass,
    stat_x, stat_z, lse8, t8, mass, t_x, t_z,
    grad_t, row_send, row_x, row_xsend, row_z, row_fin,
    code_own, code_send, code_core, code_ysend, code_y,
    book_sem, es_s, es_r, ef_s, ef_r, sx_s, sx_r, sz_s, sz_r, ms_s, ms_r,
    tx_s, tx_r, tz_s, tz_r, rx_s, rx_r, rz_s, rz_r, rb_s, rb_r,
    cc_s, cc_r, cy_s, cy_r,
):
    rows, feats = enc.shape
    tile_rows = rows * NZH
    chunk = cbt.shape[0] // NY
    half = chunk // NC
    rb = rows // LANES
    tb = tile_rows // LANES
    nz = NZH * NZL

    dp, code = lax.axis_index("dp"), lax.axis_index("code")
    y, zh, core = dp // (NZH * NC), lax.rem(dp // NC, NZH), lax.rem(dp, NC)
    x, zl = code // NZL, lax.rem(code, NZL)
    z = zh * NZL + zl
    yc = y * NC + core

    def device(x=x, y=y, zh=zh, zl=zl, core=core):
        return ((y * NZH + zh) * NC + core, x * NZL + zl)

    def at_x(i):
        return device(x=i)

    def at_z(i):
        return device(zh=i // NZL, zl=lax.rem(i, NZL))

    def at_y(i):
        return device(y=i)

    def at_xl(i):
        return device(x=i // NZL, zl=lax.rem(i, NZL))

    def at_yc(i):
        return device(y=i // NC, core=lax.rem(i, NC))

    def book_copy(r, c):
        start = pl.multiple_of((c * NZH + lax.rem(zh + r, NZH)) * chunk, chunk)
        if r == 0:
            target = cbt.at[pl.ds(c * chunk, chunk), :]
        else:
            target = tile.at[pl.ds(c * chunk, chunk), pl.ds((r - 1) * feats, feats)]
        return pltpu.make_async_copy(
            book.at[pl.ds(start, chunk), :], target, book_sem.at[r * NY + c]
        )

    for r in range(NZH):
        for c in range(NY):
            book_copy(r, c).start()

    log = []

    barrier = pltpu.get_barrier_semaphore()
    partners = (
        [at_x(lax.rem(x + r, NX)) for r in range(1, NX)]
        + [at_z(lax.rem(z + r, nz)) for r in range(1, nz)]
        + [at_yc(lax.rem(yc + r, NY * NC)) for r in range(1, NY * NC)]
        + [device(x=lax.rem(x + r, NX), zl=1 - zl) for r in range(1, NX)]
    )
    for partner in partners:
        pl.semaphore_signal(
            barrier, inc=1, device_id=partner, device_id_type=pl.DeviceIdType.MESH
        )

    own_lanes = pl.ds(pl.multiple_of(zh * rows, LANES), rows)
    own_t = transposed(enc[...])
    et[:, own_lanes] = own_t
    eg[zh] = enc[...]

    step = 128

    def online(r, c, state):
        def body(i, state):
            top, total = state
            start = pl.multiple_of(c * chunk + i * step, step)
            if r == 0:
                codes = cbt[pl.ds(start, step), :]
            else:
                codes = tile[pl.ds(start, step), pl.ds((r - 1) * feats, feats)]
            wide = codes.astype(F32)
            squared = wide * wide
            folded = squared[:, :LANES]
            for k in range(1, feats // LANES):
                folded = folded + squared[:, k * LANES:(k + 1) * LANES]
            halved = 0.5 * jnp.sum(folded, axis=1, keepdims=True)
            if r == 0:
                hsq[pl.ds(start, step), :] = jnp.broadcast_to(halved, (step, LANES))
            scores = jnp.dot(codes, et[:, own_lanes], preferred_element_type=F32)
            logits = (scores - halved).reshape(step // 8, 8, rows)
            new_top = jnp.maximum(top, jnp.max(logits, axis=0))
            total = total * jnp.exp(top - new_top) + jnp.sum(
                jnp.exp(logits - new_top[None]), axis=0
            )
            return new_top, total

        return lax.fori_loop(0, chunk // step, body, state, unroll=True)

    slice_rows = rows // NX
    my_slice = pl.ds(pl.multiple_of(x * slice_rows, slice_rows), slice_rows)

    def e_copy(r):
        other = lax.rem(zh + r, NZH)

        def slot(i):
            return remote(
                enc.at[my_slice, :], eg.at[i, my_slice, :], es_s.at[r], es_r.at[i], device(zh=other)
            )

        return Copy(log, slot(zh), slot(other))

    def e_forward(r, q):
        other, xs = lax.rem(zh + r, NZH), lax.rem(x + q, NX)
        theirs = pl.ds(pl.multiple_of(xs * slice_rows, slice_rows), slice_rows)

        def slot(i, part):
            return remote(
                eg.at[other, part, :], eg.at[other, part, :], ef_s.at[r * NX + q],
                ef_r.at[other * NX + i], at_x(xs),
            )

        return Copy(log, slot(x, my_slice), slot(xs, theirs))

    state = (jnp.full((8, rows), -1e30, F32), jnp.zeros((8, rows), F32))
    near_first = sorted(range(1, NZH), key=lambda r: min(r, NZH - r))
    e_first = {}
    for r in range(NZH):
        if r == NZH - 1:
            pl.semaphore_wait(barrier, len(partners))
            e_first = {r: e_copy(r) for r in near_first}
        for c in range(NY):
            book_copy(r, c).wait()

        def chunks(c, state, r=r):
            return online(r, c, state)

        state = lax.fori_loop(0, NY, chunks, state)
    top8, total8 = state
    top = jnp.max(top8, axis=0, keepdims=True)
    total = jnp.sum(total8 * jnp.exp(top8 - top), axis=0, keepdims=True)

    for k in range(rb):
        stat_x[x, k:k + 1, :] = top[:, k * LANES:(k + 1) * LANES]
        stat_x[x, rb + k:rb + k + 1, :] = total[:, k * LANES:(k + 1) * LANES]
    share_sx = Share(log, stat_x, NX, x, at_x, sx_s, sx_r)


    mm_step = min(NY * chunk, 1024)

    def fill_logits(block):
        lanes = pl.ds(pl.multiple_of(block * rows, LANES), rows)

        def body(i, carry):
            at = pl.ds(pl.multiple_of(i * mm_step, mm_step), mm_step)
            scores = jnp.dot(cbt[at, :], et[:, lanes], preferred_element_type=F32)
            halved = hsq[at, :]
            for k in range(rb):
                lane = pl.ds(pl.multiple_of(block * rows + k * LANES, LANES), LANES)
                logit[at, lane] = scores[:, k * LANES:(k + 1) * LANES] - halved
            return carry

        lax.fori_loop(0, NY * chunk // mm_step, body, 0)

    fill_logits(zh)

    e_second = {}
    for r in near_first:
        e_first[r].recv()
        e_second[r] = [e_forward(r, q) for q in range(1, NX)]

    share_sx.recv()
    tops, sums = stat_x[:, 0:rb, :], stat_x[:, rb:2 * rb, :]
    top = jnp.max(tops, axis=0)
    stat_z[z, 0:rb, :] = top
    stat_z[z, rb:2 * rb, :] = jnp.sum(sums * jnp.exp(tops - top[None]), axis=0)
    share_sz = Share(log, stat_z, nz, z, at_z, sz_s, sz_r)

    for r in near_first:
        other = lax.rem(zh + r, NZH)
        for copy in e_second[r]:
            copy.recv()
        et[:, pl.ds(pl.multiple_of(other * rows, LANES), rows)] = transposed(eg[other])
        fill_logits(other)

    share_sz.recv()
    for b in range(NZH):
        tops = stat_z[b * NZL:(b + 1) * NZL, 0:rb, :]
        sums = stat_z[b * NZL:(b + 1) * NZL, rb:2 * rb, :]
        top = jnp.max(tops, axis=0)
        lse = top + jnp.log(jnp.sum(sums * jnp.exp(tops - top[None]), axis=0))
        for k in range(rb):
            lane = (b * rb + k) * LANES
            lse8[:, lane:lane + LANES] = jnp.broadcast_to(lse[k:k + 1, :], (8, LANES))

    el_step = 64
    mass_rows = chunk // LANES
    share_m = []
    for c in range(NY):
        def weigh(i, carry, c=c):
            at = pl.ds(pl.multiple_of(c * chunk + i * el_step, el_step), el_step)
            part = None
            for k in range(tb):
                lane = slice(k * LANES, (k + 1) * LANES)
                values = logit[at, lane].reshape(el_step // 8, 8, LANES)
                log_weights = (values - lse8[:, lane][None]).reshape(el_step, LANES)
                weights = jnp.exp(log_weights)
                logit[at, lane] = log_weights
                weight[at, lane] = weights
                part = weights if part is None else part + weights
            lane_sum[at, :] = part
            return carry

        lax.fori_loop(0, chunk // el_step, weigh, 0, unroll=2)
        for k in range(mass_rows):
            start = c * chunk + k * LANES
            mass[c, yc, k:k + 1, :] = jnp.sum(
                lane_sum[start:start + LANES, :].T, axis=0, keepdims=True
            )
        share_m.append(Share(log, mass.at[c], NY * NC, yc, at_yc, ms_s.at[c], ms_r.at[c]))

    t_sum = jnp.zeros((8, tile_rows), F32)
    for c in range(NY):
        share_m[c].recv()
        logs = jnp.log(jnp.sum(mass[c], axis=0) / rows_total)
        for k in range(mass_rows):
            start = c * chunk + k * LANES
            log_mass[start:start + LANES, :] = jnp.broadcast_to(
                logs[k:k + 1, :], (LANES, LANES)
            ).T

        def shape(i, t_sum, c=c):
            at = pl.ds(pl.multiple_of(c * chunk + i * el_step, el_step), el_step)
            logs = log_mass[at, :]
            parts = []
            for k in range(tb):
                lane = slice(k * LANES, (k + 1) * LANES)
                q = weight[at, lane] * (logs - logit[at, lane])
                logit[at, lane] = q
                parts.append(jnp.sum(q.reshape(el_step // 8, 8, LANES), axis=0))
            return t_sum + jnp.concatenate(parts, axis=1)

        t_sum = lax.fori_loop(0, chunk // el_step, shape, t_sum, unroll=2)
    t_row = jnp.sum(t_sum, axis=0, keepdims=True)
    for k in range(tb):
        t_x[x, k:k + 1, :] = t_row[:, k * LANES:(k + 1) * LANES]
    share_tx = Share(log, t_x, NX, x, at_x, tx_s, tx_r)

    turn_step = min(NY * chunk, 256)

    def turn_codes(i, carry):
        at = pl.ds(pl.multiple_of(i * turn_step, turn_step), turn_step)
        ct[:, at] = transposed(cbt[at, :])
        return carry

    lax.fori_loop(0, NY * chunk // turn_step, turn_codes, 0)

    share_tx.recv()
    t_z[z] = jnp.sum(t_x[...], axis=0)
    Share(log, t_z, nz, z, at_z, tz_s, tz_r).recv()
    t_all = jnp.sum(t_z[...], axis=0)
    for k in range(tb):
        t8[:, k * LANES:(k + 1) * LANES] = jnp.broadcast_to(t_all[k:k + 1, :], (8, LANES))

    partner = 1 - core
    g_step = min(half, 256)

    def grad_tile(start):
        at = pl.ds(start, g_step)
        sums = jnp.zeros((g_step, LANES), F32)
        for k in range(tb):
            lane = slice(k * LANES, (k + 1) * LANES)
            q = logit[at, lane].reshape(g_step // 8, 8, LANES)
            w = weight[at, lane].reshape(g_step // 8, 8, LANES)
            g = (q - w * t8[:, lane][None]).reshape(g_step, LANES)
            sums = sums + g
            tile[at, lane] = g.astype(BF16)
        lane_sum[at, :] = sums

    def code_grad(start):
        at = pl.ds(start, g_step)
        totals = jnp.sum(lane_sum[at, :], axis=1, keepdims=True)
        pulled = jnp.dot(
            tile[at, :], eg[...].reshape(tile_rows, feats), preferred_element_type=F32
        )
        return pulled - totals * cbt[at, :].astype(F32)

    def code_compute(r, fill, multiply):
        first = lax.rem(y + r, NY) * chunk

        def body(k, carry):
            theirs = pl.multiple_of(first + partner * half + k * g_step, g_step)
            ours = pl.multiple_of(first + core * half + k * g_step, g_step)
            to = pl.ds(pl.multiple_of(k * g_step, g_step), g_step)
            if fill:
                grad_tile(theirs)
            if multiply:
                code_send[r, to, :] = code_grad(theirs).astype(BF16)
            if fill:
                grad_tile(ours)
            if multiply:
                code_own[r, to, :] = code_grad(ours)
            return carry

        lax.fori_loop(0, half // g_step, body, 0)

    def code_exchange(r):
        copy = remote(
            code_send.at[r], code_core.at[r], cc_s.at[r], cc_r.at[r], device(core=partner)
        )
        return Copy(log, copy, copy)

    def code_forward(r):
        core_copies[r].recv()
        code_ysend[r] = (code_own[r] + code_core[r].astype(F32)).astype(BF16)
        other = lax.rem(y + r, NY)

        def slot(i):
            return remote(
                code_ysend.at[r], code_y.at[i], cy_s.at[r], cy_r.at[i], at_y(other)
            )

        return Copy(log, slot(y), slot(other))

    far_first = sorted(range(1, NY), key=lambda r: -min(r, NY - r)) + [0]
    core_copies, y_copies = {}, {}
    for i, r in enumerate(far_first):
        code_compute(r, True, r != 0)
        if r:
            core_copies[r] = code_exchange(r)
        if i >= 1:
            y_copies[far_first[i - 1]] = code_forward(far_first[i - 1])

    fx = feats // NX
    x_slice = pl.ds(pl.multiple_of(x * fx, fx), fx)

    def row_compute(r):
        lanes = pl.ds(pl.multiple_of(lax.rem(zh + r, NZH) * rows, LANES), rows)
        value = jnp.dot(ct[...], tile[:, lanes], preferred_element_type=F32)
        grad_t[r] = value
        row_send[r] = value.astype(BF16)
        copies = []
        for q in range(1, NX):
            other = lax.rem(x + q, NX)

            def slot(i, q=q, other=other):
                part = pl.ds(pl.multiple_of(other * fx, fx), fx)
                return remote(
                    row_send.at[r, part, :], row_x.at[i, r], rx_s.at[r, q], rx_r.at[r, i],
                    at_x(other),
                )

            copies.append(Copy(log, slot(x), slot(other)))
        return copies

    def row_forward(r):
        for copy in x_copies[r]:
            copy.recv()
        total = grad_t[r, x_slice, :]
        for q in range(1, NX):
            total = total + row_x[lax.rem(x + q, NX), r].astype(F32)
        if r == 0:
            return total
        row_xsend[r] = total.astype(BF16)
        other = lax.rem(zh + r, NZH)

        def slot(i):
            return remote(row_xsend.at[r], row_z.at[i], rz_s.at[r], rz_r.at[i], device(zh=other))

        z_copies.append(Copy(log, slot(zh), slot(other)))

    far_blocks = sorted(range(1, NZH), key=lambda r: -min(r, NZH - r)) + [0]
    x_copies, z_copies = {}, []
    for i, r in enumerate(far_blocks):
        x_copies[r] = row_compute(r)
        if i >= 2:
            row_forward(far_blocks[i - 2])
    code_compute(0, False, True)
    core_copies[0] = code_exchange(0)
    row_forward(far_blocks[-2])
    total = row_forward(far_blocks[-1])
    for copy in z_copies:
        copy.recv()
    for r in range(1, NZH):
        total = total + row_z[lax.rem(zh + r, NZH)].astype(F32)
    slot = x * NZL + zl
    row_fin[slot] = total.astype(BF16)
    share_rb = Share(log, row_fin, NX * NZL, slot, at_xl, rb_s, rb_r)

    core_copies[0].recv()
    codes_out[...] = code_own[0] + code_core[0].astype(F32)
    for r in far_first[:-1]:
        y_copies[r].recv()
        codes_out[...] += code_y[lax.rem(y + r, NY)].astype(F32)

    share_rb.recv()
    for k in range(NX):
        part = row_fin[k * NZL].astype(F32)
        for j in range(1, NZL):
            part = part + row_fin[k * NZL + j].astype(F32)
        rows_out[:, k * fx:(k + 1) * fx] = part.T

    for copy in log:
        copy.finish()


def body(encoded, codebook):
    rows, feats = encoded.shape
    shard = codebook.shape[0]
    tile_codes = shard // NZH
    chunk = tile_codes // NY
    half = chunk // NC
    tile_rows = rows * NZH
    rb, tb = rows // LANES, tile_rows // LANES
    nz = NZH * NZL
    fx = feats // NX
    rows_total = rows * lax.axis_size("dp")
    dma = pltpu.SemaphoreType.DMA
    scratch = [
        pltpu.VMEM((tile_codes, feats), BF16),
        pltpu.VMEM((feats, tile_rows), BF16),
        pltpu.VMEM((NZH, rows, feats), BF16),
        pltpu.VMEM((feats, tile_codes), BF16),
        pltpu.VMEM((tile_codes, LANES), F32),
        pltpu.VMEM((tile_codes, tile_rows), F32),
        pltpu.VMEM((tile_codes, tile_rows), F32),
        pltpu.VMEM((tile_codes, tile_rows), BF16),
        pltpu.VMEM((tile_codes, LANES), F32),
        pltpu.VMEM((tile_codes, LANES), F32),
        pltpu.VMEM((NX, 2 * rb, LANES), F32),
        pltpu.VMEM((nz, 2 * rb, LANES), F32),
        pltpu.VMEM((8, tile_rows), F32),
        pltpu.VMEM((8, tile_rows), F32),
        pltpu.VMEM((NY, NY * NC, chunk // LANES, LANES), F32),
        pltpu.VMEM((NX, tb, LANES), F32),
        pltpu.VMEM((nz, tb, LANES), F32),
        pltpu.VMEM((NZH, feats, rows), F32),
        pltpu.VMEM((NZH, feats, rows), BF16),
        pltpu.VMEM((NX, NZH, fx, rows), BF16),
        pltpu.VMEM((NZH, fx, rows), BF16),
        pltpu.VMEM((NZH, fx, rows), BF16),
        pltpu.VMEM((NX * NZL, fx, rows), BF16),
        pltpu.VMEM((NY, half, feats), F32),
        pltpu.VMEM((NY, half, feats), BF16),
        pltpu.VMEM((NY, half, feats), BF16),
        pltpu.VMEM((NY, half, feats), BF16),
        pltpu.VMEM((NY, half, feats), BF16),
        dma((NZH * NY,)),
        dma((NZH,)), dma((NZH,)), dma((NZH * NX,)), dma((NZH * NX,)),
        dma((NX,)), dma((NX,)), dma((nz,)), dma((nz,)),
        dma((NY, NY * NC)), dma((NY, NY * NC)),
        dma((NX,)), dma((NX,)), dma((nz,)), dma((nz,)),
        dma((NZH, NX)), dma((NZH, NX)), dma((NZH,)), dma((NZH,)),
        dma((NX * NZL,)), dma((NX * NZL,)),
        dma((NY,)), dma((NY,)), dma((NY,)), dma((NY,)),
    ]
    vmem = pl.BlockSpec(memory_space=pltpu.VMEM)
    return pl.pallas_call(
        functools.partial(kernel, float(rows_total)),
        out_shape=(
            jax.ShapeDtypeStruct((rows, feats), F32),
            jax.ShapeDtypeStruct((half, feats), F32),
        ),
        in_specs=[vmem, pl.BlockSpec(memory_space=pl.ANY)],
        out_specs=(vmem, vmem),
        scratch_shapes=scratch,
        compiler_params=pltpu.CompilerParams(
            collective_id=0, has_side_effects=True, vmem_limit_bytes=67_000_000
        ),
    )(encoded, codebook)


def solution(mesh):
    placed = (P("dp", None), P("code", None))
    return jax.shard_map(
        body,
        mesh=mesh,
        in_specs=placed,
        out_specs=(P("dp", None), P(("code", "dp"), None)),
        check_vma=False,
    )
```

```python
import functools

import jax
import jax.numpy as jnp
from jax import lax
from jax.experimental import pallas as pl
from jax.experimental.pallas import tpu as pltpu
from jax.sharding import PartitionSpec as P

NX, NY, NZH, NZL, NC = 4, 4, 4, 2, 2
F32, BF16 = jnp.float32, jnp.bfloat16
LANES = 128


def remote(src, dst, send_sem, recv_sem, device):
    return pltpu.make_async_remote_copy(
        src_ref=src,
        dst_ref=dst,
        send_sem=send_sem,
        recv_sem=recv_sem,
        device_id=device,
        device_id_type=pl.DeviceIdType.MESH,
    )


class Copy:
    def __init__(self, log, outgoing, incoming):
        self.outgoing, self.incoming, self.arrived = outgoing, incoming, False
        outgoing.start()
        log.append(self)

    def recv(self):
        self.incoming.wait_recv()
        self.arrived = True

    def finish(self):
        if not self.arrived:
            self.recv()
        self.outgoing.wait_send()


class Share:
    def __init__(self, log, buf, n, me, device_of, send_sem, recv_sem):
        self.copies = []
        for r in range(1, n):
            there = lax.rem(me + r, n)

            def slot(i, r=r, there=there):
                return remote(
                    buf.at[i], buf.at[i], send_sem.at[r], recv_sem.at[i], device_of(there)
                )

            self.copies.append(Copy(log, slot(me), slot(there)))

    def recv(self):
        for copy in self.copies:
            copy.recv()


def transposed(block):
    return block.astype(F32).T.astype(BF16)


def kernel(
    rows_total,
    enc, book, rows_out, codes_out,
    cbt, et, eg, ct, hsq, logit, weight, tile, lane_sum, log_mass,
    stat_x, stat_z, lse8, t8, mass, t_x, t_z,
    grad_t, row_send, row_x, row_xsend, row_z, row_fin,
    code_own, code_send, code_core, code_ysend, code_y,
    book_sem, es_s, es_r, ef_s, ef_r, sx_s, sx_r, sz_s, sz_r, ms_s, ms_r,
    tx_s, tx_r, tz_s, tz_r, rx_s, rx_r, rz_s, rz_r, rb_s, rb_r,
    cc_s, cc_r, cy_s, cy_r,
):
    rows, feats = enc.shape
    tile_rows = rows * NZH
    chunk = cbt.shape[0] // NY
    half = chunk // NC
    rb = rows // LANES
    tb = tile_rows // LANES
    nz = NZH * NZL

    dp, code = lax.axis_index("dp"), lax.axis_index("code")
    y, zh, core = dp // (NZH * NC), lax.rem(dp // NC, NZH), lax.rem(dp, NC)
    x, zl = code // NZL, lax.rem(code, NZL)
    z = zh * NZL + zl
    yc = y * NC + core

    def device(x=x, y=y, zh=zh, zl=zl, core=core):
        return ((y * NZH + zh) * NC + core, x * NZL + zl)

    def at_x(i):
        return device(x=i)

    def at_z(i):
        return device(zh=i // NZL, zl=lax.rem(i, NZL))

    def at_y(i):
        return device(y=i)

    def at_xl(i):
        return device(x=i // NZL, zl=lax.rem(i, NZL))

    def at_yc(i):
        return device(y=i // NC, core=lax.rem(i, NC))

    def book_copy(r, c):
        start = pl.multiple_of((c * NZH + lax.rem(zh + r, NZH)) * chunk, chunk)
        if r == 0:
            target = cbt.at[pl.ds(c * chunk, chunk), :]
        else:
            target = tile.at[pl.ds(c * chunk, chunk), pl.ds((r - 1) * feats, feats)]
        return pltpu.make_async_copy(
            book.at[pl.ds(start, chunk), :], target, book_sem.at[r * NY + c]
        )

    for c in range(NY):
        book_copy(0, c).start()

    log = []

    barrier = pltpu.get_barrier_semaphore()
    partners = (
        [at_x(lax.rem(x + r, NX)) for r in range(1, NX)]
        + [at_z(lax.rem(z + r, nz)) for r in range(1, nz)]
        + [at_yc(lax.rem(yc + r, NY * NC)) for r in range(1, NY * NC)]
        + [device(x=lax.rem(x + r, NX), zl=1 - zl) for r in range(1, NX)]
    )
    for partner in partners:
        pl.semaphore_signal(
            barrier, inc=1, device_id=partner, device_id_type=pl.DeviceIdType.MESH
        )

    own_lanes = pl.ds(pl.multiple_of(zh * rows, LANES), rows)
    own_t = transposed(enc[...])
    et[:, own_lanes] = own_t
    eg[zh] = enc[...]

    step = 128

    def online(r, c, state):
        def body(i, state):
            top, total = state
            start = pl.multiple_of(c * chunk + i * step, step)
            if r == 0:
                codes = cbt[pl.ds(start, step), :]
            else:
                codes = tile[pl.ds(start, step), pl.ds((r - 1) * feats, feats)]
            wide = codes.astype(F32)
            squared = wide * wide
            folded = squared[:, :LANES]
            for k in range(1, feats // LANES):
                folded = folded + squared[:, k * LANES:(k + 1) * LANES]
            halved = 0.5 * jnp.sum(folded, axis=1, keepdims=True)
            if r == 0:
                hsq[pl.ds(start, step), :] = jnp.broadcast_to(halved, (step, LANES))
            scores = jnp.dot(codes, et[:, own_lanes], preferred_element_type=F32)
            logits = (scores - halved).reshape(step // 8, 8, rows)
            new_top = jnp.maximum(top, jnp.max(logits, axis=0))
            total = total * jnp.exp(top - new_top) + jnp.sum(
                jnp.exp(logits - new_top[None]), axis=0
            )
            return new_top, total

        return lax.fori_loop(0, chunk // step, body, state, unroll=True)

    slice_rows = rows // NX
    my_slice = pl.ds(pl.multiple_of(x * slice_rows, slice_rows), slice_rows)

    def e_copy(r):
        other = lax.rem(zh + r, NZH)
        part = my_slice if 2 * r == NZH else pl.ds(0, rows)

        def slot(i):
            return remote(
                enc.at[part, :], eg.at[i, part, :], es_s.at[r], es_r.at[i], device(zh=other)
            )

        return Copy(log, slot(zh), slot(other))

    def e_forward(r, q):
        other, xs = lax.rem(zh + r, NZH), lax.rem(x + q, NX)
        theirs = pl.ds(pl.multiple_of(xs * slice_rows, slice_rows), slice_rows)

        def slot(i, part):
            return remote(
                eg.at[other, part, :], eg.at[other, part, :], ef_s.at[r * NX + q],
                ef_r.at[other * NX + i], at_x(xs),
            )

        return Copy(log, slot(x, my_slice), slot(xs, theirs))

    state = (jnp.full((8, rows), -1e30, F32), jnp.zeros((8, rows), F32))
    far_then_near = sorted(range(1, NZH), key=lambda r: -min(r, NZH - r))
    far_rows = far_then_near[0]
    e_first = {}
    for r in range(NZH):
        if r == NZH - 1:
            pl.semaphore_wait(barrier, len(partners))
            e_first = {k: e_copy(k) for k in far_then_near}
        for c in range(NY):
            book_copy(r, c).wait()
        for c in range(NY if r < NZH - 1 else 0):
            book_copy(r + 1, c).start()

        def chunks(c, state, r=r):
            return online(r, c, state)

        state = lax.fori_loop(0, NY, chunks, state)
    top8, total8 = state
    top = jnp.max(top8, axis=0, keepdims=True)
    total = jnp.sum(total8 * jnp.exp(top8 - top), axis=0, keepdims=True)

    for k in range(rb):
        stat_x[x, k:k + 1, :] = top[:, k * LANES:(k + 1) * LANES]
        stat_x[x, rb + k:rb + k + 1, :] = total[:, k * LANES:(k + 1) * LANES]
    share_sx = Share(log, stat_x, NX, x, at_x, sx_s, sx_r)


    mm_step = min(NY * chunk, 1024)

    def fill_logits(block):
        lanes = pl.ds(pl.multiple_of(block * rows, LANES), rows)

        def body(i, carry):
            at = pl.ds(pl.multiple_of(i * mm_step, mm_step), mm_step)
            scores = jnp.dot(cbt[at, :], et[:, lanes], preferred_element_type=F32)
            halved = hsq[at, :]
            for k in range(rb):
                lane = pl.ds(pl.multiple_of(block * rows + k * LANES, LANES), LANES)
                logit[at, lane] = scores[:, k * LANES:(k + 1) * LANES] - halved
            return carry

        lax.fori_loop(0, NY * chunk // mm_step, body, 0)

    fill_logits(zh)

    e_first[far_rows].recv()
    e_second = [e_forward(far_rows, q) for q in range(1, NX)]

    share_sx.recv()
    tops, sums = stat_x[:, 0:rb, :], stat_x[:, rb:2 * rb, :]
    top = jnp.max(tops, axis=0)
    stat_z[z, 0:rb, :] = top
    stat_z[z, rb:2 * rb, :] = jnp.sum(sums * jnp.exp(tops - top[None]), axis=0)
    share_sz = Share(log, stat_z, nz, z, at_z, sz_s, sz_r)

    for r in far_then_near[1:] + [far_rows]:
        other = lax.rem(zh + r, NZH)
        for copy in e_second if r == far_rows else [e_first[r]]:
            copy.recv()
        et[:, pl.ds(pl.multiple_of(other * rows, LANES), rows)] = transposed(eg[other])
        fill_logits(other)

    share_sz.recv()
    for b in range(NZH):
        tops = stat_z[b * NZL:(b + 1) * NZL, 0:rb, :]
        sums = stat_z[b * NZL:(b + 1) * NZL, rb:2 * rb, :]
        top = jnp.max(tops, axis=0)
        lse = top + jnp.log(jnp.sum(sums * jnp.exp(tops - top[None]), axis=0))
        for k in range(rb):
            lane = (b * rb + k) * LANES
            lse8[:, lane:lane + LANES] = jnp.broadcast_to(lse[k:k + 1, :], (8, LANES))

    el_step = 64
    mass_rows = chunk // LANES
    share_m = []
    for c in range(NY):
        def weigh(i, carry, c=c):
            at = pl.ds(pl.multiple_of(c * chunk + i * el_step, el_step), el_step)
            part = None
            for k in range(tb):
                lane = slice(k * LANES, (k + 1) * LANES)
                values = logit[at, lane].reshape(el_step // 8, 8, LANES)
                log_weights = (values - lse8[:, lane][None]).reshape(el_step, LANES)
                weights = jnp.exp(log_weights)
                logit[at, lane] = log_weights
                weight[at, lane] = weights
                part = weights if part is None else part + weights
            lane_sum[at, :] = part
            return carry

        lax.fori_loop(0, chunk // el_step, weigh, 0, unroll=2)
        for k in range(mass_rows):
            start = c * chunk + k * LANES
            mass[c, yc, k:k + 1, :] = jnp.sum(
                lane_sum[start:start + LANES, :].T, axis=0, keepdims=True
            )
        share_m.append(Share(log, mass.at[c], NY * NC, yc, at_yc, ms_s.at[c], ms_r.at[c]))

    t_sum = jnp.zeros((8, tile_rows), F32)
    for c in range(NY):
        share_m[c].recv()
        logs = jnp.log(jnp.sum(mass[c], axis=0) / rows_total)
        for k in range(mass_rows):
            start = c * chunk + k * LANES
            log_mass[start:start + LANES, :] = jnp.broadcast_to(
                logs[k:k + 1, :], (LANES, LANES)
            ).T

        def shape(i, t_sum, c=c):
            at = pl.ds(pl.multiple_of(c * chunk + i * el_step, el_step), el_step)
            logs = log_mass[at, :]
            parts = []
            for k in range(tb):
                lane = slice(k * LANES, (k + 1) * LANES)
                q = weight[at, lane] * (logs - logit[at, lane])
                logit[at, lane] = q
                parts.append(jnp.sum(q.reshape(el_step // 8, 8, LANES), axis=0))
            return t_sum + jnp.concatenate(parts, axis=1)

        t_sum = lax.fori_loop(0, chunk // el_step, shape, t_sum, unroll=2)
    t_row = jnp.sum(t_sum, axis=0, keepdims=True)
    for k in range(tb):
        t_x[x, k:k + 1, :] = t_row[:, k * LANES:(k + 1) * LANES]
    share_tx = Share(log, t_x, NX, x, at_x, tx_s, tx_r)

    turn_step = min(NY * chunk, 256)

    def turn_codes(i, carry):
        at = pl.ds(pl.multiple_of(i * turn_step, turn_step), turn_step)
        ct[:, at] = transposed(cbt[at, :])
        return carry

    lax.fori_loop(0, NY * chunk // turn_step, turn_codes, 0)

    share_tx.recv()
    t_z[z] = jnp.sum(t_x[...], axis=0)
    Share(log, t_z, nz, z, at_z, tz_s, tz_r).recv()
    t_all = jnp.sum(t_z[...], axis=0)
    for k in range(tb):
        t8[:, k * LANES:(k + 1) * LANES] = jnp.broadcast_to(t_all[k:k + 1, :], (8, LANES))

    partner = 1 - core
    g_step = min(half, 256)

    def grad_tile(start):
        at = pl.ds(start, g_step)
        sums = jnp.zeros((g_step, LANES), F32)
        for k in range(tb):
            lane = slice(k * LANES, (k + 1) * LANES)
            q = logit[at, lane].reshape(g_step // 8, 8, LANES)
            w = weight[at, lane].reshape(g_step // 8, 8, LANES)
            g = (q - w * t8[:, lane][None]).reshape(g_step, LANES)
            sums = sums + g
            tile[at, lane] = g.astype(BF16)
        lane_sum[at, :] = sums

    def code_grad(start):
        at = pl.ds(start, g_step)
        totals = jnp.sum(lane_sum[at, :], axis=1, keepdims=True)
        pulled = jnp.dot(
            tile[at, :], eg[...].reshape(tile_rows, feats), preferred_element_type=F32
        )
        return pulled - totals * cbt[at, :].astype(F32)

    def code_compute(r, fill, multiply):
        first = lax.rem(y + r, NY) * chunk

        def body(k, carry):
            theirs = pl.multiple_of(first + partner * half + k * g_step, g_step)
            ours = pl.multiple_of(first + core * half + k * g_step, g_step)
            to = pl.ds(pl.multiple_of(k * g_step, g_step), g_step)
            if fill:
                grad_tile(theirs)
            if multiply:
                code_send[r, to, :] = code_grad(theirs).astype(BF16)
            if fill:
                grad_tile(ours)
            if multiply:
                code_own[r, to, :] = code_grad(ours)
            return carry

        lax.fori_loop(0, half // g_step, body, 0)

    def code_exchange(r):
        copy = remote(
            code_send.at[r], code_core.at[r], cc_s.at[r], cc_r.at[r], device(core=partner)
        )
        return Copy(log, copy, copy)

    def code_forward(r):
        core_copies[r].recv()
        code_ysend[r] = (code_own[r] + code_core[r].astype(F32)).astype(BF16)
        other = lax.rem(y + r, NY)

        def slot(i):
            return remote(
                code_ysend.at[r], code_y.at[i], cy_s.at[r], cy_r.at[i], at_y(other)
            )

        return Copy(log, slot(y), slot(other))

    far_first = sorted(range(1, NY), key=lambda r: -min(r, NY - r)) + [0]
    core_copies, y_copies = {}, {}

    fx = feats // NX
    x_slice = pl.ds(pl.multiple_of(x * fx, fx), fx)

    def row_compute(r):
        lanes = pl.ds(pl.multiple_of(lax.rem(zh + r, NZH) * rows, LANES), rows)
        value = jnp.dot(ct[...], tile[:, lanes], preferred_element_type=F32)
        grad_t[r] = value
        row_send[r] = value.astype(BF16)
        copies = []
        for q in range(1, NX):
            other = lax.rem(x + q, NX)

            def slot(i, q=q, other=other):
                part = pl.ds(pl.multiple_of(other * fx, fx), fx)
                return remote(
                    row_send.at[r, part, :], row_x.at[i, r], rx_s.at[r, q], rx_r.at[r, i],
                    at_x(other),
                )

            copies.append(Copy(log, slot(x), slot(other)))
        return copies

    def row_forward(r):
        for copy in x_copies[r]:
            copy.recv()
        total = grad_t[r, x_slice, :]
        for q in range(1, NX):
            total = total + row_x[lax.rem(x + q, NX), r].astype(F32)
        if r == 0:
            return total
        row_xsend[r] = total.astype(BF16)
        other = lax.rem(zh + r, NZH)

        def slot(i):
            return remote(row_xsend.at[r], row_z.at[i], rz_s.at[r], rz_r.at[i], device(zh=other))

        z_copies.append(Copy(log, slot(zh), slot(other)))

    far_blocks = sorted(range(1, NZH), key=lambda r: -min(r, NZH - r)) + [0]
    x_copies, z_copies = {}, []
    early, late = far_first[:-1][:2], far_first[:-1][2:]
    for i, r in enumerate(early):
        code_compute(r, True, True)
        core_copies[r] = code_exchange(r)
        if i >= 1:
            y_copies[early[i - 1]] = code_forward(early[i - 1])
    for r in late + [0]:
        code_compute(r, True, False)
    for i, r in enumerate(far_blocks):
        x_copies[r] = row_compute(r)
        if i == 0:
            y_copies[early[-1]] = code_forward(early[-1])
        if i == 1:
            for k in late:
                code_compute(k, False, True)
                core_copies[k] = code_exchange(k)
        if i >= 2:
            row_forward(far_blocks[i - 2])
        if i == 2:
            for k in late:
                y_copies[k] = code_forward(k)
    code_compute(0, False, True)
    core_copies[0] = code_exchange(0)
    row_forward(far_blocks[-2])
    total = row_forward(far_blocks[-1])
    for copy in z_copies:
        copy.recv()
    for r in range(1, NZH):
        total = total + row_z[lax.rem(zh + r, NZH)].astype(F32)
    slot = x * NZL + zl
    row_fin[slot] = total.astype(BF16)
    share_rb = Share(log, row_fin, NX * NZL, slot, at_xl, rb_s, rb_r)

    core_copies[0].recv()
    codes_out[...] = code_own[0] + code_core[0].astype(F32)
    for r in far_first[:-1]:
        y_copies[r].recv()
        codes_out[...] += code_y[lax.rem(y + r, NY)].astype(F32)

    share_rb.recv()
    for k in range(NX):
        part = row_fin[k * NZL].astype(F32)
        for j in range(1, NZL):
            part = part + row_fin[k * NZL + j].astype(F32)
        rows_out[:, k * fx:(k + 1) * fx] = part.T

    for copy in log:
        copy.finish()


def hand_over(rows_in, codes_in, rows_out, codes_out):
    rows_out[...] = rows_in[...]
    codes_out[...] = codes_in[...]


def body(encoded, codebook):
    rows, feats = encoded.shape
    shard = codebook.shape[0]
    tile_codes = shard // NZH
    chunk = tile_codes // NY
    half = chunk // NC
    tile_rows = rows * NZH
    rb, tb = rows // LANES, tile_rows // LANES
    nz = NZH * NZL
    fx = feats // NX
    rows_total = rows * lax.axis_size("dp")
    dma = pltpu.SemaphoreType.DMA
    scratch = [
        pltpu.VMEM((tile_codes, feats), BF16),
        pltpu.VMEM((feats, tile_rows), BF16),
        pltpu.VMEM((NZH, rows, feats), BF16),
        pltpu.VMEM((feats, tile_codes), BF16),
        pltpu.VMEM((tile_codes, LANES), F32),
        pltpu.VMEM((tile_codes, tile_rows), F32),
        pltpu.VMEM((tile_codes, tile_rows), F32),
        pltpu.VMEM((tile_codes, tile_rows), BF16),
        pltpu.VMEM((tile_codes, LANES), F32),
        pltpu.VMEM((tile_codes, LANES), F32),
        pltpu.VMEM((NX, 2 * rb, LANES), F32),
        pltpu.VMEM((nz, 2 * rb, LANES), F32),
        pltpu.VMEM((8, tile_rows), F32),
        pltpu.VMEM((8, tile_rows), F32),
        pltpu.VMEM((NY, NY * NC, chunk // LANES, LANES), F32),
        pltpu.VMEM((NX, tb, LANES), F32),
        pltpu.VMEM((nz, tb, LANES), F32),
        pltpu.VMEM((NZH, feats, rows), F32),
        pltpu.VMEM((NZH, feats, rows), BF16),
        pltpu.VMEM((NX, NZH, fx, rows), BF16),
        pltpu.VMEM((NZH, fx, rows), BF16),
        pltpu.VMEM((NZH, fx, rows), BF16),
        pltpu.VMEM((NX * NZL, fx, rows), BF16),
        pltpu.VMEM((NY, half, feats), F32),
        pltpu.VMEM((NY, half, feats), BF16),
        pltpu.VMEM((NY, half, feats), BF16),
        pltpu.VMEM((NY, half, feats), BF16),
        pltpu.VMEM((NY, half, feats), BF16),
        dma((NZH * NY,)),
        dma((NZH,)), dma((NZH,)), dma((NZH * NX,)), dma((NZH * NX,)),
        dma((NX,)), dma((NX,)), dma((nz,)), dma((nz,)),
        dma((NY, NY * NC)), dma((NY, NY * NC)),
        dma((NX,)), dma((NX,)), dma((nz,)), dma((nz,)),
        dma((NZH, NX)), dma((NZH, NX)), dma((NZH,)), dma((NZH,)),
        dma((NX * NZL,)), dma((NX * NZL,)),
        dma((NY,)), dma((NY,)), dma((NY,)), dma((NY,)),
    ]
    vmem = pl.BlockSpec(memory_space=pltpu.VMEM)
    shapes = (
        jax.ShapeDtypeStruct((rows, feats), F32),
        jax.ShapeDtypeStruct((half, feats), F32),
    )
    results = pl.pallas_call(
        functools.partial(kernel, float(rows_total)),
        out_shape=shapes,
        in_specs=[vmem, pl.BlockSpec(memory_space=pl.ANY)],
        out_specs=(vmem, vmem),
        scratch_shapes=scratch,
        compiler_params=pltpu.CompilerParams(
            collective_id=0, has_side_effects=True, vmem_limit_bytes=67_000_000
        ),
    )(encoded, codebook)
    return pl.pallas_call(
        hand_over, out_shape=shapes, in_specs=[vmem, vmem], out_specs=(vmem, vmem)
    )(*results)


def solution(mesh):
    placed = (P("dp", None), P("code", None))
    return jax.shard_map(
        body,
        mesh=mesh,
        in_specs=placed,
        out_specs=(P("dp", None), P(("code", "dp"), None)),
        check_vma=False,
    )
```
